32 devices in a mesh: group: 2 (over y), replica: 16 (over z, x, core).
Axes of the slice: x: 2, y: 2, z: 4, core: 2. Of those that a mesh axis runs over, the one named last changes fastest.
Arguments:
- tokens: bfloat16 [6144, 960], P(('group', 'replica')), may hold values from -6 to 6
- seq_lens: int32 [32, 4], P(('group', 'replica')), may hold values from 1 to 96, 192 in all within a row
- cotangent: bfloat16 [6144, 960], P(('group', 'replica')), may hold values from -6 to 6
- norm1_gain: bfloat16 [960], P('group'), may hold values from 0.25 to 1.75
- w_query: bfloat16 [960, 960], P('group'), may hold values from -0.1875 to 0.1875
- key_weight: bfloat16 [960, 320], P('group'), may hold values from -0.1875 to 0.1875
- value_weight: bfloat16 [960, 320], P('group'), may hold values from -0.1875 to 0.1875
- w_output: bfloat16 [960, 960], P('group'), may hold values from -0.5 to 0.5
- norm2_gain: bfloat16 [960], P('group'), may hold values from 0.25 to 1.75
- w_gate: bfloat16 [960, 2560], P(None, 'group'), may hold values from -0.1875 to 0.1875
- w_up: bfloat16 [960, 2560], P(None, 'group'), may hold values from -0.1875 to 0.1875
- w_down: bfloat16 [2560, 960], P('group'), may hold values from -0.125 to 0.125
Outputs:
- layer_out: bfloat16 [6144, 960], P(('group', 'replica'))
- tokens_grad: float32 [6144, 960], P(('group', 'replica'))
- norm1_gain_grad: float32 [960], P('group')
- w_query_grad: float32 [960, 960], P('group')
- w_key_grad: float32 [960, 320], P('group')
- w_value_grad: float32 [960, 320], P('group')
- w_output_grad: float32 [960, 960], P('group')
- norm2_gain_grad: float32 [960], P('group')
- w_gate_grad: float32 [960, 2560], P(None, 'group')
- w_up_grad: float32 [960, 2560], P(None, 'group')
- w_down_grad: float32 [2560, 960], P('group')
The draws below stay inside these ranges and needn't reach their ends.
Inputs may be any that keep to these rules, and one draw needn't show every extreme that they name: `seq_lens`: each device's row holds the lengths of its 4 sequences, which add up to 192; the longest in every row is 96.
All inputs are finite; a program needn't handle non-finite values.
Results may differ from the reference program's by a relative error of at most 0.023.
Values may be sent and summed in bfloat16 or wider, within the bound.
A program may use at most 192 MiB of HBM per device.

```python
import math
import jax
import jax.numpy as jnp
import numpy as np
from jax import lax

MODEL_WIDTH = 960
QUERY_HEADS = 15
KEY_VALUE_HEADS = 5
HEAD_SIZE = 64
FF = 2560
TOK_DEV = 192
SEQS_DEV = 4
SEQ_MAX = 96
TOKENS = 6144
N_GROUP = 2
N_REPLICA = 16


def levels(rng, shape, split, smallest, largest):
    def one(dim, parts):
        draws = jax.random.uniform(jax.random.fold_in(jax.random.fold_in(rng, 6), dim), (parts,), jnp.float32, smallest / len(split), largest / len(split))
        return jnp.repeat(jnp.exp(draws), shape[dim] // parts).reshape((-1,) + (1,) * (len(shape) - dim - 1))

    factor_of = one(*split[0])
    for cut in split[1:]:
        factor_of = factor_of * one(*cut)
    return factor_of


def profile(amount, total, limit, slope):
    loads = [(1 << 20) // math.isqrt(rank ** slope) + 1 for rank in range(2, amount + 1)]
    spare, given = total - limit - (amount - 1), [1] * (amount - 1)
    while spare > 0:
        movable = [i for i in range(amount - 1) if given[i] < limit]
        mass, budget = sum([loads[i] for i in movable]), spare
        for i in movable:
            extra = min(limit - given[i], max(1, budget * loads[i] // mass), spare)
            given[i] = given[i] + extra
            spare = spare - extra
    return np.array([limit] + given)


def ragged_sizes(stream_key, count, total, bound, lean):
    if count == 2:
        one = jax.random.randint(stream_key, (), max(1, total - bound), min(bound, total - 1) + 1)
        return jnp.stack([one, total - one])
    tallies = jnp.asarray(profile(count, total, bound, lean), jnp.int32)
    twos = (count - 1) // 2
    source_of, sink = tallies[1:1 + 2 * twos:2], tallies[2:2 + 2 * twos:2]
    room = jnp.minimum(source_of - 1, bound - sink)
    passed = jax.random.randint(jax.random.fold_in(stream_key, 1), (twos,), 0, 1 << 20) % (room + 1)
    tallies = tallies.at[1:1 + 2 * twos:2].set(source_of - passed).at[2:2 + 2 * twos:2].set(sink + passed)
    return tallies[jax.random.permutation(jax.random.fold_in(stream_key, 2), count)]


def normal_values(key, shape, deviation, limit, pieces=(), kind=jnp.bfloat16):
    drawn = deviation * jax.random.normal(key, shape, jnp.float32)
    if pieces:
        drawn = drawn * levels(key, shape, pieces, -0.22, 0.18)
    return jnp.clip(drawn, -limit, limit).astype(kind)


def setup_inputs(seed: int = 0) -> dict:
    splits = jax.random.split(jax.random.key(seed), 13)
    return {
        "tokens": normal_values(splits[0], (TOKENS, MODEL_WIDTH), 1.0, 6.0, ((0, 32),)),
        "seq_lens": jax.vmap(lambda own: ragged_sizes(own, SEQS_DEV, TOK_DEV, SEQ_MAX, 2))(jax.random.split(splits[1], (N_GROUP * N_REPLICA))).reshape((N_GROUP * N_REPLICA, SEQS_DEV)).astype(jnp.int32),
        "cotangent": normal_values(splits[2], (TOKENS, MODEL_WIDTH), 1.0, 6.0, ((0, 32),)),
        "norm1_gain": jnp.clip(1.0 + 0.15 * jax.random.normal(splits[3], (MODEL_WIDTH,), jnp.float32), 0.25, 1.75).astype(jnp.bfloat16),
        "w_query": normal_values(splits[4], (MODEL_WIDTH, QUERY_HEADS * HEAD_SIZE), MODEL_WIDTH ** -0.5, 0.1875, ((0, 2),)),
        "key_weight": normal_values(splits[5], (MODEL_WIDTH, KEY_VALUE_HEADS * HEAD_SIZE), MODEL_WIDTH ** -0.5, 0.1875, ((0, 2),)),
        "value_weight": normal_values(splits[6], (MODEL_WIDTH, KEY_VALUE_HEADS * HEAD_SIZE), MODEL_WIDTH ** -0.5, 0.1875, ((0, 2),)),
        "w_output": normal_values(splits[7], (QUERY_HEADS * HEAD_SIZE, MODEL_WIDTH), (QUERY_HEADS * HEAD_SIZE // 8) ** -0.5, 0.5, ((0, 2),)),
        "norm2_gain": jnp.clip(1.0 + 0.15 * jax.random.normal(splits[8], (MODEL_WIDTH,), jnp.float32), 0.25, 1.75).astype(jnp.bfloat16),
        "w_gate": normal_values(splits[9], (MODEL_WIDTH, FF), MODEL_WIDTH ** -0.5, 0.1875, ((1, 2),)),
        "w_up": normal_values(splits[10], (MODEL_WIDTH, FF), MODEL_WIDTH ** -0.5, 0.1875, ((1, 2),)),
        "w_down": normal_values(splits[11], (FF, MODEL_WIDTH), FF ** -0.5, 0.125, ((0, 2),)),
    }


EPS = 1e-05

def matrix_product(left, right):
    return jnp.dot(left, right, preferred_element_type=jnp.float32)

def left_t_product(left, right):
    return lax.dot_general(left, right, (((0,), (0,)), ((), ())), preferred_element_type=jnp.float32)

def right_t_product(left, right):
    return lax.dot_general(left, right, (((1,), (1,)), ((), ())), preferred_element_type=jnp.float32)

def wide_einsum(form, left, right):
    return jnp.einsum(form, left.astype(jnp.float32), right.astype(jnp.float32))

def sequence_tables(lengths, token_count):
    ends = jnp.cumsum(lengths).astype(jnp.int32)
    starts = ends - lengths
    indices = jnp.arange(token_count, dtype=jnp.int32)
    seq_of = lax.optimization_barrier(jnp.sum((indices[:, None] >= ends[None, :]).astype(jnp.int32), axis=1))
    onehot = (seq_of[:, None] == jnp.arange(lengths.shape[0], dtype=jnp.int32)[None, :]).astype(jnp.int32)
    position = indices - lax.optimization_barrier(jnp.sum(onehot * starts[None, :], axis=1))
    half_dim = HEAD_SIZE // 2
    freqs = 10000.0 ** (-(jnp.arange(half_dim, dtype=jnp.float32) * 2.0 / HEAD_SIZE))
    angles = position.astype(jnp.float32)[:, None] * freqs[None, :]
    visible = (seq_of[:, None] == seq_of[None, :]) & (indices[None, :] <= indices[:, None])
    return (jnp.cos(angles), jnp.sin(angles), visible)

def apply_rotary(values, cosine_table, sine_table):
    half_dim = values.shape[-1] // 2
    first_half = values[..., :half_dim]
    second_half = values[..., half_dim:]
    cos_b = cosine_table[:, None, :]
    sin_b = sine_table[:, None, :]
    return jnp.concatenate([first_half * cos_b - second_half * sin_b, second_half * cos_b + first_half * sin_b], axis=-1)

def rotary_backward(values, cosine_table, sine_table):
    half_dim = values.shape[-1] // 2
    first_half = values[..., :half_dim]
    second_half = values[..., half_dim:]
    cos_b = cosine_table[:, None, :]
    sin_b = sine_table[:, None, :]
    return jnp.concatenate([first_half * cos_b + second_half * sin_b, second_half * cos_b - first_half * sin_b], axis=-1)

def rms_scale(resid, gain):
    inv_rms = lax.rsqrt(lax.optimization_barrier(jnp.mean(resid * resid, axis=-1, keepdims=True)) + EPS)
    return ((resid * inv_rms * gain.astype(jnp.float32)).astype(jnp.bfloat16), inv_rms)

def rms_back(d_normed, resid, inv_rms, gain):
    scaled = d_normed * gain.astype(jnp.float32)
    d_resid = inv_rms * scaled - resid * inv_rms ** 3 * lax.optimization_barrier(jnp.mean(scaled * resid, axis=-1, keepdims=True))
    d_gain = lax.optimization_barrier(jnp.sum(d_normed * resid * inv_rms, axis=0))
    return (d_resid, d_gain)

def masked_scores(query_rotated, key_rotated, visible):
    token_count = query_rotated.shape[0]
    query_grouped = query_rotated.reshape(token_count, KEY_VALUE_HEADS, QUERY_HEADS // KEY_VALUE_HEADS, HEAD_SIZE)
    scores = wide_einsum('qhgd,khd->hgqk', query_grouped, key_rotated) * (1.0 / math.sqrt(HEAD_SIZE))
    return (jnp.where(visible[None, None], scores, -1e+30), query_grouped)

def attention(query_rotated, key_rotated, value_row_block, visible):
    token_count = query_rotated.shape[0]
    scores, query_grouped = masked_scores(query_rotated, key_rotated, visible)
    top = lax.optimization_barrier(jnp.max(scores, axis=-1, keepdims=True))
    expo = jnp.exp(scores - top)
    total = lax.optimization_barrier(jnp.sum(expo, axis=-1, keepdims=True))
    log_total = top + jnp.log(total)
    probs = (expo / total).astype(jnp.bfloat16)
    mixed = wide_einsum('hgqk,khd->qhgd', probs, value_row_block)
    return (mixed.reshape(token_count, QUERY_HEADS * HEAD_SIZE).astype(jnp.bfloat16), log_total)

def attention_back(query_rotated, key_rotated, value_row_block, attention_mixture, mixture_gradient, log_total, visible):
    token_count = query_rotated.shape[0]
    scores, query_grouped = masked_scores(query_rotated, key_rotated, visible)
    weights_f = jnp.exp(scores - log_total)
    probs = weights_f.astype(jnp.bfloat16)
    mixture_gradient_grouped = mixture_gradient.reshape(token_count, KEY_VALUE_HEADS, QUERY_HEADS // KEY_VALUE_HEADS, HEAD_SIZE)
    mixture_grouped = attention_mixture.reshape(token_count, KEY_VALUE_HEADS, QUERY_HEADS // KEY_VALUE_HEADS, HEAD_SIZE)
    value_gradient = wide_einsum('hgqk,qhgd->khd', probs, mixture_gradient_grouped)
    d_probs = wide_einsum('qhgd,khd->hgqk', mixture_gradient_grouped, value_row_block)
    delta = wide_einsum('qhgd,qhgd->hgq', mixture_gradient_grouped, mixture_grouped)[..., None]
    d_scores = (weights_f * (d_probs - delta) * (1.0 / math.sqrt(HEAD_SIZE))).astype(jnp.bfloat16)
    d_query = wide_einsum('hgqk,khd->qhgd', d_scores, key_rotated).reshape(token_count, QUERY_HEADS, HEAD_SIZE)
    key_gradient = wide_einsum('hgqk,qhgd->khd', d_scores, query_grouped)
    return (d_query, key_gradient, value_gradient)

def forward_pass(block, lengths, weights):
    gain_one, w_query, key_weight, value_weight, w_output, gain_two, w_gate, w_up, w_down = weights
    token_count = block.shape[0]
    cosine_table, sine_table, visible = sequence_tables(lengths, token_count)
    resid_in = block.astype(jnp.float32)
    first_normed_input, inv_rms_one = rms_scale(resid_in, gain_one)
    query_rotated = apply_rotary(matrix_product(first_normed_input, w_query).reshape(token_count, QUERY_HEADS, HEAD_SIZE), cosine_table, sine_table).astype(jnp.bfloat16)
    key_rotated = apply_rotary(matrix_product(first_normed_input, key_weight).reshape(token_count, KEY_VALUE_HEADS, HEAD_SIZE), cosine_table, sine_table).astype(jnp.bfloat16)
    value_row_block = matrix_product(first_normed_input, value_weight).astype(jnp.bfloat16).reshape(token_count, KEY_VALUE_HEADS, HEAD_SIZE)
    attention_mixture, log_total = attention(query_rotated, key_rotated, value_row_block, visible)
    resid_mid = resid_in + matrix_product(attention_mixture, w_output)
    normed_two, inv_rms_two = rms_scale(resid_mid, gain_two)
    gate_pre = matrix_product(normed_two, w_gate)
    up_pre = matrix_product(normed_two, w_up)
    hidden = (jax.nn.silu(gate_pre) * up_pre).astype(jnp.bfloat16)
    resid_out = resid_mid + matrix_product(hidden, w_down)
    saved = (resid_in, first_normed_input, inv_rms_one, query_rotated, key_rotated, value_row_block, attention_mixture, log_total, resid_mid, normed_two, inv_rms_two, gate_pre, up_pre, hidden, cosine_table, sine_table, visible)
    return (resid_out.astype(jnp.bfloat16), saved)

def mlp_backward(d_out, saved, weights):
    gain_one, w_query, key_weight, value_weight, w_output, gain_two, w_gate, w_up, w_down = weights
    resid_mid, normed_two, inv_rms_two, gate_pre, up_pre, hidden = saved[8:14]
    d_out_b = d_out.astype(jnp.bfloat16)
    grad_down = left_t_product(hidden, d_out_b)
    d_hidden = right_t_product(d_out_b, w_down)
    sigma = jax.nn.sigmoid(gate_pre)
    d_gate = (d_hidden * up_pre * sigma * (1.0 + gate_pre * (1.0 - sigma))).astype(jnp.bfloat16)
    d_up = (d_hidden * gate_pre * sigma).astype(jnp.bfloat16)
    grad_gate = left_t_product(normed_two, d_gate)
    grad_up = left_t_product(normed_two, d_up)
    d_normed_two = right_t_product(d_gate, w_gate) + right_t_product(d_up, w_up)
    d_resid_part, grad_gain_two = rms_back(d_normed_two, resid_mid, inv_rms_two, gain_two)
    return (d_out + d_resid_part, (grad_gain_two, grad_gate, grad_up, grad_down))

def attn_backward(d_resid_mid, saved, weights):
    gain_one, w_query, key_weight, value_weight, w_output, gain_two, w_gate, w_up, w_down = weights
    resid_in, first_normed_input, inv_rms_one, query_rotated, key_rotated, value_row_block, attention_mixture, log_total = saved[:8]
    cosine_table, sine_table, visible = saved[14:]
    token_count = resid_in.shape[0]
    d_mid_b = d_resid_mid.astype(jnp.bfloat16)
    grad_output = left_t_product(attention_mixture, d_mid_b)
    mixture_gradient = right_t_product(d_mid_b, w_output).astype(jnp.bfloat16)
    d_query, key_gradient, value_gradient = attention_back(query_rotated, key_rotated, value_row_block, attention_mixture, mixture_gradient, log_total, visible)
    d_query_b = rotary_backward(d_query, cosine_table, sine_table).reshape(token_count, QUERY_HEADS * HEAD_SIZE).astype(jnp.bfloat16)
    key_gradient_block = rotary_backward(key_gradient, cosine_table, sine_table).reshape(token_count, KEY_VALUE_HEADS * HEAD_SIZE).astype(jnp.bfloat16)
    value_gradient_block = value_gradient.reshape(token_count, KEY_VALUE_HEADS * HEAD_SIZE).astype(jnp.bfloat16)
    grad_query = left_t_product(first_normed_input, d_query_b)
    grad_key = left_t_product(first_normed_input, key_gradient_block)
    grad_value = left_t_product(first_normed_input, value_gradient_block)
    d_normed_one = right_t_product(d_query_b, w_query) + right_t_product(key_gradient_block, key_weight) + right_t_product(value_gradient_block, value_weight)
    d_resid_part, grad_gain_one = rms_back(d_normed_one, resid_in, inv_rms_one, gain_one)
    return (d_resid_mid + d_resid_part, (grad_gain_one, grad_query, grad_key, grad_value, grad_output))

def reference(tokens, seq_lens, cotangent, norm1_gain, w_query, key_weight, value_weight, w_output, norm2_gain, w_gate, w_up, w_down):
    weights = (norm1_gain, w_query, key_weight, value_weight, w_output, norm2_gain, w_gate, w_up, w_down)
    blocks = N_GROUP * N_REPLICA
    token_blocks = tokens.reshape(blocks, TOK_DEV, MODEL_WIDTH)
    cot_blocks = cotangent.reshape(blocks, TOK_DEV, MODEL_WIDTH)
    zeros = tuple((jnp.zeros(weight.shape, jnp.float32) for weight in weights))

    def step(totals, item):
        block, lengths, cot_block = item
        layer_block, saved = forward_pass(block, lengths, weights)
        d_resid_mid, mlp_grads = mlp_backward(cot_block.astype(jnp.float32), saved, weights)
        d_tokens, attn_grads = attn_backward(d_resid_mid, saved, weights)
        grads = attn_grads + mlp_grads
        rounded = tuple((lax.optimization_barrier(part.astype(jnp.bfloat16)).astype(jnp.float32) for part in grads))
        return (tuple((total + part for total, part in zip(totals, rounded))), (layer_block, d_tokens))
    totals, (outs, d_tokens) = lax.scan(step, zeros, (token_blocks, seq_lens, cot_blocks))
    factor = 1.0 / math.sqrt(float(TOKENS))
    return (outs.reshape(TOKENS, MODEL_WIDTH), d_tokens.reshape(TOKENS, MODEL_WIDTH), totals[0] * factor, totals[1] * factor, totals[2] * factor, totals[3] * factor, totals[4] * factor, totals[5] * factor, totals[6] * factor, totals[7] * factor, totals[8] * factor)
```

```python
import functools
import math

import jax
import jax.numpy as jnp
from jax import lax
from jax.experimental import pallas as pl
from jax.experimental.pallas import tpu as pltpu
from jax.sharding import PartitionSpec as P

QUERY_HEADS = 15
KEY_VALUE_HEADS = 5
HEAD_SIZE = 64


EPS = 1e-05


def matrix_product(left, right):
    return jnp.dot(left, right, preferred_element_type=jnp.float32)


def left_t_product(left, right):
    return lax.dot_general(
        left, right, (((0,), (0,)), ((), ())), preferred_element_type=jnp.float32
    )


def right_t_product(left, right):
    return lax.dot_general(
        left, right, (((1,), (1,)), ((), ())), preferred_element_type=jnp.float32
    )


def mixed_einsum(form, left, right):
    return jnp.einsum(form, left, right, preferred_element_type=jnp.float32)


def sequence_tables(lengths, token_count):
    ends = jnp.cumsum(lengths)
    starts = ends - lengths
    indices = jnp.arange(token_count, dtype=jnp.int32)
    seq_of = jnp.sum((indices[:, None] >= ends[None, :]).astype(jnp.int32), axis=1)
    onehot = (seq_of[:, None] == jnp.arange(lengths.shape[0], dtype=jnp.int32)[None, :]).astype(
        jnp.int32
    )
    position = indices - jnp.sum(onehot * starts[None, :], axis=1)
    half_dim = HEAD_SIZE // 2
    freqs = 10000.0 ** (-(jnp.arange(half_dim, dtype=jnp.float32) * 2.0 / HEAD_SIZE))
    angles = position.astype(jnp.float32)[:, None] * freqs[None, :]
    visible = (seq_of[:, None] == seq_of[None, :]) & (indices[None, :] <= indices[:, None])
    return (jnp.cos(angles), jnp.sin(angles), visible)


def apply_rotary(values, cosine_table, sine_table):
    half_dim = values.shape[-1] // 2
    first_half = values[..., :half_dim]
    second_half = values[..., half_dim:]
    cos_b = cosine_table[:, None, :]
    sin_b = sine_table[:, None, :]
    return jnp.concatenate(
        [first_half * cos_b - second_half * sin_b, second_half * cos_b + first_half * sin_b],
        axis=-1,
    )


def rotary_backward(values, cosine_table, sine_table):
    half_dim = values.shape[-1] // 2
    first_half = values[..., :half_dim]
    second_half = values[..., half_dim:]
    cos_b = cosine_table[:, None, :]
    sin_b = sine_table[:, None, :]
    return jnp.concatenate(
        [first_half * cos_b + second_half * sin_b, second_half * cos_b - first_half * sin_b],
        axis=-1,
    )


def rms_scale(resid, gain):
    inv_rms = lax.rsqrt(jnp.mean(resid * resid, axis=-1, keepdims=True) + EPS)
    return ((resid * inv_rms * gain.astype(jnp.float32)).astype(jnp.bfloat16), inv_rms)


def rms_back(d_normed, resid, inv_rms, gain):
    scaled = d_normed * gain.astype(jnp.float32)
    d_resid = inv_rms * scaled - resid * inv_rms**3 * jnp.mean(
        scaled * resid, axis=-1, keepdims=True
    )
    d_gain = jnp.sum(d_normed * resid * inv_rms, axis=0)
    return (d_resid, d_gain)


def masked_scores(query_rotated, key_rotated, visible):
    token_count = query_rotated.shape[0]
    query_grouped = query_rotated.reshape(
        token_count, KEY_VALUE_HEADS, QUERY_HEADS // KEY_VALUE_HEADS, HEAD_SIZE
    )
    scores = mixed_einsum("qhgd,khd->hgqk", query_grouped, key_rotated) * (
        1.0 / math.sqrt(HEAD_SIZE)
    )
    return (jnp.where(visible[None, None], scores, -1e30), query_grouped)


def attention(query_rotated, key_rotated, value_row_block, visible):
    token_count = query_rotated.shape[0]
    scores, query_grouped = masked_scores(query_rotated, key_rotated, visible)
    top = jnp.max(scores, axis=-1, keepdims=True)
    expo = jnp.exp(scores - top)
    total = jnp.sum(expo, axis=-1, keepdims=True)
    log_total = top + jnp.log(total)
    probs = (expo / total).astype(jnp.bfloat16)
    mixed = mixed_einsum("hgqk,khd->qhgd", probs, value_row_block)
    return (mixed.reshape(token_count, QUERY_HEADS * HEAD_SIZE).astype(jnp.bfloat16), log_total)


def attention_back(
    query_rotated,
    key_rotated,
    value_row_block,
    attention_mixture,
    mixture_gradient,
    log_total,
    visible,
):
    token_count = query_rotated.shape[0]
    scores, query_grouped = masked_scores(query_rotated, key_rotated, visible)
    weights_f = jnp.exp(scores - log_total)
    probs = weights_f.astype(jnp.bfloat16)
    mixture_gradient_grouped = mixture_gradient.reshape(
        token_count, KEY_VALUE_HEADS, QUERY_HEADS // KEY_VALUE_HEADS, HEAD_SIZE
    )
    mixture_grouped = attention_mixture.reshape(
        token_count, KEY_VALUE_HEADS, QUERY_HEADS // KEY_VALUE_HEADS, HEAD_SIZE
    )
    value_gradient = mixed_einsum("hgqk,qhgd->khd", probs, mixture_gradient_grouped)
    d_probs = mixed_einsum("qhgd,khd->hgqk", mixture_gradient_grouped, value_row_block)
    delta = mixed_einsum("qhgd,qhgd->hgq", mixture_gradient_grouped, mixture_grouped)[..., None]
    d_scores = (weights_f * (d_probs - delta) * (1.0 / math.sqrt(HEAD_SIZE))).astype(jnp.bfloat16)
    d_query = mixed_einsum("hgqk,khd->qhgd", d_scores, key_rotated).reshape(
        token_count, QUERY_HEADS, HEAD_SIZE
    )
    key_gradient = mixed_einsum("hgqk,qhgd->khd", d_scores, query_grouped)
    return (d_query, key_gradient, value_gradient)


def from_member(values, shift):
    size = lax.axis_size("group")
    return lax.ppermute(values, "group", [(j, (j - shift) % size) for j in range(size)])


def to_member(values, shift):
    size = lax.axis_size("group")
    return lax.ppermute(values, "group", [(j, (j + shift) % size) for j in range(size)])


def group_tokens(values):
    others = [from_member(values, k) for k in range(1, lax.axis_size("group"))]
    return jnp.concatenate([values] + others, axis=0)


def group_scatter_sum(parts, token_count):
    total = parts[:token_count]
    for k in range(1, lax.axis_size("group")):
        part = parts[k * token_count : (k + 1) * token_count].astype(jnp.bfloat16)
        total = total + to_member(part, k).astype(jnp.float32)
    return total


def in_group_order(blocks, axis):
    size = len(blocks)
    me = lax.axis_index("group")
    if size == 2:
        first = jnp.where(me == 0, blocks[0], blocks[1])
        second = jnp.where(me == 0, blocks[1], blocks[0])
        return jnp.concatenate([first, second], axis=axis)
    stacked = jnp.roll(jnp.stack(blocks), me, axis=0)
    return jnp.concatenate([stacked[i] for i in range(size)], axis=axis)


def gather_rows(block):
    half = block.shape[0] // 2
    core = lax.rem(lax.axis_index("replica"), 2)
    pairs = [(i, i ^ 1) for i in range(lax.axis_size("replica"))]
    mine = lax.dynamic_slice_in_dim(block, core * half, half, axis=0)
    blocks = [block]
    for k in range(1, lax.axis_size("group")):
        piece = from_member(mine, k)
        pair = lax.ppermute(piece, "replica", pairs)
        first = jnp.where(core == 0, piece, pair)
        second = jnp.where(core == 0, pair, piece)
        blocks.append(jnp.concatenate([first, second], axis=0))
    return in_group_order(blocks, 0)


UNIT = 32
LAG = 3


def replica_layout(replicas):
    chips = replicas // 2
    outer = 4 if chips % 4 == 0 else (2 if chips % 2 == 0 else 1)
    return outer, chips // outer


def sum_kernel(dims, gate_ref, up_ref, down_ref, attn_ref, out_ref, *scratch):
    groups, outer, inner, per_dense, per_attn = dims
    (
        core_in,
        part,
        low_in,
        high_in,
        inner_in,
        group_out,
        group_in,
        core_send,
        core_recv,
        inner_send,
        inner_recv,
        up_send,
        low_recv,
        high_recv,
        fin_low_send,
        fin_high_send,
        fin_inner_send,
        fin_core_send,
        fin_recv,
        fin_core_recv,
        group_send,
        group_recv,
    ) = scratch
    dense = (gate_ref, up_ref, down_ref)
    first_attn = len(dense) * per_dense
    units = first_attn + per_attn
    me = lax.axis_index("replica")
    mine = lax.axis_index("group")
    core = lax.rem(me, 2)
    inner_at = lax.rem(me // 2, inner)
    outer_at = me // (2 * inner)

    def replica_of(o, i, c):
        return {"replica": (o * inner + i) * 2 + c}

    def rows(u):
        return pl.ds(pl.multiple_of(u * UNIT, UNIT), UNIT)

    def pair_rows(u, c):
        return pl.ds(pl.multiple_of((u * 2 + c) * UNIT, UNIT), UNIT)

    def copy(source, target, send, recv, device):
        return pltpu.make_async_remote_copy(
            src_ref=source,
            dst_ref=target,
            send_sem=send,
            recv_sem=recv,
            device_id=device,
            device_id_type=pl.DeviceIdType.MESH,
        )

    other_core = replica_of(outer_at, inner_at, 1 - core)

    def core_copy(source, slot):
        return copy(
            source, core_in.at[rows(slot)], core_send.at[slot], core_recv.at[slot], other_core
        )

    def dense_copy(a, j):
        return core_copy(dense[a].at[pair_rows(j, 1 - core)], a * per_dense + j)

    def attn_slot(owner, j):
        return first_attn + owner * per_attn + j

    def attn_copy(owner, j):
        return core_copy(attn_ref.at[owner, pair_rows(j, 1 - core)], attn_slot(owner, j))

    def group_copy(k, j):
        owner = lax.rem(mine + k, groups)
        return copy(
            group_out.at[k - 1, rows(j)],
            group_in.at[k - 1, rows(j)],
            group_send.at[k - 1, j],
            group_recv.at[k - 1, j],
            {"group": owner},
        )

    def inner_copy(u, owner):
        k = lax.rem(inner_at - owner + inner, inner) - 1
        return copy(
            part.at[rows(u)],
            inner_in.at[k, rows(u)],
            inner_send.at[u],
            inner_recv.at[k, u],
            replica_of(outer_at, owner, core),
        )

    def up_copy(u, step):
        buffer, recv = (low_in, low_recv) if step > 0 else (high_in, high_recv)
        return copy(
            part.at[rows(u)],
            buffer.at[rows(u)],
            up_send.at[u],
            recv.at[u],
            replica_of(outer_at + step, inner_at, core),
        )

    def final_copy(u, send, device):
        place = out_ref.at[pair_rows(u, core)]
        return copy(place, place, send, fin_recv.at[u], device)

    def final_low(u):
        return final_copy(u, fin_low_send.at[u], replica_of(outer_at - 1, inner_at, core))

    def final_high(u):
        return final_copy(u, fin_high_send.at[u], replica_of(outer_at + 1, inner_at, core))

    def final_inner(u, k):
        peer = lax.rem(inner_at + k, inner)
        return final_copy(u, fin_inner_send.at[k - 1, u], replica_of(outer_at, peer, core))

    def final_core(u, c):
        place = out_ref.at[pair_rows(u, c)]
        return copy(place, place, fin_core_send.at[u], fin_core_recv.at[u], other_core)

    def wide(values):
        return values.astype(jnp.float32)

    def add_in(u, arrived):
        part[rows(u)] = (wide(part[rows(u)]) + wide(arrived)).astype(part.dtype)

    def role(u):
        turn, slot = u // 5, lax.rem(u, 5)
        late = slot // 3
        count = turn * 3 + slot
        owner_early = lax.rem(count, inner)
        owner_late = lax.rem(slot + turn, inner)
        root_early = max(outer // 2 - 1, 0) + lax.rem(count // inner, min(outer, 2))
        root_late = lax.rem(turn, outer)
        early = 1 - late
        owner = early * owner_early + late * owner_late
        root = early * root_early + late * root_late
        return early, owner, root

    def facts(u):
        early, owner, root = role(u)
        owns = inner_at == owner
        in_tree = (early == 0) | owns
        at_root = outer_at == root
        tallest = jnp.maximum(root, outer - 1 - root)
        below, above = outer_at < root, outer_at > root
        height = (
            below.astype(jnp.int32) * outer_at
            + above.astype(jnp.int32) * (outer - 1 - outer_at)
            + at_root.astype(jnp.int32) * tallest
        )
        distance = jnp.abs(outer_at - root)
        up_step = early + height
        final_step = 1 + tallest
        down_step = final_step + distance + (1 - owns.astype(jnp.int32))
        return {
            "early": early == 1,
            "owner": owner,
            "owns": owns,
            "in_tree": in_tree,
            "at_root": at_root,
            "below": below,
            "above": above,
            "up_step": up_step,
            "final_step": final_step,
            "down_step": down_step,
            "from_low": (outer_at > 0) & (outer_at <= root),
            "from_high": (outer_at < outer - 1) & (outer_at >= root),
            "sends_inner": (inner_at != owner) & ((early == 1) | at_root),
        }

    barrier = pltpu.get_barrier_semaphore()

    def greet(device):
        pl.semaphore_signal(
            barrier, inc=1, device_id=device, device_id_type=pl.DeviceIdType.MESH
        )

    greet(other_core)
    for k in range(1, inner):
        greet(replica_of(outer_at, lax.rem(inner_at + k, inner), core))
    for k in range(1, groups):
        greet({"group": lax.rem(mine + k, groups)})

    @pl.when(outer_at > 0)
    def _():
        greet(replica_of(outer_at - 1, inner_at, core))

    @pl.when(outer_at < outer - 1)
    def _():
        greet(replica_of(outer_at + 1, inner_at, core))

    ends = (outer_at > 0).astype(jnp.int32) + (outer_at < outer - 1).astype(jnp.int32)
    pl.semaphore_wait(barrier, 1 + (inner - 1) + (groups - 1) + ends)

    @pl.loop(0, per_dense)
    def _(j):
        dense_copy(0, j).start()

    @pl.loop(0, per_attn)
    def _(j):
        for k in range(1, groups):
            attn_copy(lax.rem(mine + k, groups), j).start()

    for a in range(1, len(dense)):

        @pl.loop(0, per_dense)
        def _(j):
            dense_copy(a, j).start()

    @pl.loop(0, per_attn)
    def _(j):
        attn_copy(mine, j).start()

    def first_sum(u):
        for a in range(len(dense)):

            @pl.when((u >= a * per_dense) & (u < (a + 1) * per_dense))
            def _():
                j = u - a * per_dense
                dense_copy(a, j).wait_recv()
                total = wide(dense[a][pair_rows(j, core)]) + wide(core_in[rows(u)])
                part[rows(u)] = total.astype(part.dtype)

        @pl.when(u >= first_attn)
        def _():
            j = u - first_attn
            attn_copy(mine, j).wait_recv()
            total = wide(attn_ref[mine, pair_rows(j, core)]) + wide(
                core_in[rows(attn_slot(mine, j))]
            )
            for k in range(1, groups):
                group_copy(k, j).wait_recv()
                total = total + wide(group_in[k - 1, rows(j)])
            part[rows(u)] = total.astype(part.dtype)

    def to_groups(j):
        for k in range(1, groups):
            owner = lax.rem(mine + k, groups)
            attn_copy(owner, j).wait_recv()
            total = wide(attn_ref[owner, pair_rows(j, core)]) + wide(
                core_in[rows(attn_slot(owner, j))]
            )
            group_out[k - 1, rows(j)] = total.astype(group_out.dtype)
        for k in range(1, groups):
            group_copy(k, j).start()

    def distribute(u, f):
        @pl.when(f["from_low"] & f["in_tree"])
        def _():
            final_low(u).start()

        @pl.when(f["from_high"] & f["in_tree"])
        def _():
            final_high(u).start()

        @pl.when(f["owns"] & (f["early"] | f["at_root"]))
        def _():
            for k in range(1, inner):
                final_inner(u, k).start()

        final_core(u, core).start()

    def gather_inner(u):
        for k in range(1, inner):
            inner_arrival(u, k).wait_recv()
            add_in(u, inner_in[k - 1, rows(u)])

    def inner_arrival(u, k):
        return copy(
            part.at[rows(u)],
            inner_in.at[k - 1, rows(u)],
            inner_send.at[u],
            inner_recv.at[k - 1, u],
            other_core,
        )

    def finish(u, f):
        out_ref[pair_rows(u, core)] = part[rows(u)]
        distribute(u, f)

    def act(u, step):
        f = facts(u)

        @pl.when(step == 0)
        def _():
            first_sum(u)

            @pl.when(f["early"] & (inner_at != f["owner"]))
            def _():
                inner_copy(u, f["owner"]).start()

        @pl.when(f["in_tree"] & (step == f["up_step"]))
        def _():
            @pl.when(f["early"])
            def _():
                gather_inner(u)

            @pl.when(f["from_low"])
            def _():
                up_copy_from(u, 1).wait_recv()
                add_in(u, low_in[rows(u)])

            @pl.when(f["from_high"])
            def _():
                up_copy_from(u, -1).wait_recv()
                add_in(u, high_in[rows(u)])

            @pl.when(f["below"])
            def _():
                up_copy(u, 1).start()

            @pl.when(f["above"])
            def _():
                up_copy(u, -1).start()

            @pl.when(f["at_root"] & jnp.logical_not(f["early"]) & (inner_at != f["owner"]))
            def _():
                inner_copy(u, f["owner"]).start()

        @pl.when(f["at_root"] & f["owns"] & (step == f["final_step"]))
        def _():
            @pl.when(jnp.logical_not(f["early"]))
            def _():
                gather_inner(u)

            finish(u, f)

        @pl.when(jnp.logical_not(f["at_root"] & f["owns"]) & (step == f["down_step"]))
        def _():
            final_core_arrival(u).wait_recv()
            distribute(u, f)

    def up_copy_from(u, step):
        buffer, recv = (low_in, low_recv) if step > 0 else (high_in, high_recv)
        return copy(part.at[rows(u)], buffer.at[rows(u)], up_send.at[u], recv.at[u], other_core)

    def final_core_arrival(u):
        place = out_ref.at[pair_rows(u, core)]
        return copy(place, place, fin_core_send.at[u], fin_recv.at[u], other_core)

    steps = 2 * outer + 2
    first_group_turn = 6

    @pl.loop(0, units + (steps - 1) * LAG)
    def _(t):
        @pl.loop(0, steps)
        def _(step):
            u = t - step * LAG

            @pl.when((u >= 0) & (u < units))
            def _():
                act(u, step)

        @pl.when((t >= first_group_turn) & (t < first_group_turn + per_attn))
        def _():
            to_groups(t - first_group_turn)

    @pl.loop(0, units)
    def _(u):
        f = facts(u)
        final_core(u, 1 - core).wait_recv()
        final_core(u, core).wait_send()

        @pl.when(f["sends_inner"])
        def _():
            inner_copy(u, f["owner"]).wait_send()

        @pl.when(f["in_tree"] & jnp.logical_not(f["at_root"]))
        def _():
            up_copy_from(u, 1).wait_send()

        @pl.when(f["from_low"] & f["in_tree"])
        def _():
            final_low(u).wait_send()

        @pl.when(f["from_high"] & f["in_tree"])
        def _():
            final_high(u).wait_send()

        @pl.when(f["owns"] & (f["early"] | f["at_root"]))
        def _():
            for k in range(1, inner):
                final_inner(u, k).wait_send()

    @pl.loop(0, per_dense)
    def _(j):
        for a in range(len(dense)):
            dense_copy(a, j).wait_send()

    @pl.loop(0, per_attn)
    def _(j):
        for k in range(groups):
            attn_copy(lax.rem(mine + k, groups), j).wait_send()
        for k in range(1, groups):
            group_copy(k, j).wait_send()


def summed_over_replicas(gate, up, down, attn):
    groups = lax.axis_size("group")
    outer, inner = replica_layout(lax.axis_size("replica"))
    columns = gate.shape[1]
    per_dense = gate.shape[0] // (2 * UNIT)
    per_attn = attn.shape[1] // (2 * UNIT)
    units = 3 * per_dense + per_attn
    core_slots = 3 * per_dense + groups * per_attn
    dims = (groups, outer, inner, per_dense, per_attn)

    def held(count, *lead):
        return pltpu.VMEM((*lead, count * UNIT, columns), gate.dtype)

    sems = pltpu.SemaphoreType.DMA
    others = max(inner - 1, 1)
    peers = max(groups - 1, 1)
    vmem = pl.BlockSpec(memory_space=pltpu.VMEM)
    return pl.pallas_call(
        functools.partial(sum_kernel, dims),
        out_shape=jax.ShapeDtypeStruct((units * 2 * UNIT, columns), gate.dtype),
        in_specs=[vmem] * 4,
        out_specs=vmem,
        scratch_shapes=[
            held(core_slots),
            held(units),
            held(units),
            held(units),
            held(units, others),
            held(per_attn, peers),
            held(per_attn, peers),
            sems((core_slots,)),
            sems((core_slots,)),
            sems((units,)),
            sems((others, units)),
            sems((units,)),
            sems((units,)),
            sems((units,)),
            sems((units,)),
            sems((units,)),
            sems((others, units)),
            sems((units,)),
            sems((units,)),
            sems((units,)),
            sems((peers, per_attn)),
            sems((peers, per_attn)),
        ],
        compiler_params=pltpu.CompilerParams(
            collective_id=0, has_side_effects=True, vmem_limit_bytes=67043328
        ),
        name="replica_sum",
    )(gate, up, down, attn)


def local(
    tokens,
    seq_lens,
    cotangent,
    norm1_gain,
    w_query,
    key_weight,
    value_weight,
    w_output,
    norm2_gain,
    w_gate,
    w_up,
    w_down,
):
    token_count, width = tokens.shape
    group = lax.axis_index("group")
    half_width = w_query.shape[0]
    query_width = w_query.shape[1]
    key_width = key_weight.shape[1]
    gains_mine = jnp.stack([norm1_gain, norm2_gain])
    group_size = lax.axis_size("group")
    gains = in_group_order(
        [gains_mine] + [from_member(gains_mine, k) for k in range(1, group_size)], 1
    )
    gain_one, gain_two = gains[0], gains[1]
    qkv_weight = gather_rows(jnp.concatenate([w_query, key_weight, value_weight], axis=1))
    out_weight = gather_rows(w_output)
    d_out = cotangent.astype(jnp.float32)
    d_out_pair = group_tokens(cotangent)

    cosine_table, sine_table, visible = sequence_tables(seq_lens[0], token_count)
    resid_in = tokens.astype(jnp.float32)
    normed_one, inv_rms_one = rms_scale(resid_in, gain_one)
    qkv = matrix_product(normed_one, qkv_weight)
    query_rotated = apply_rotary(
        qkv[:, :query_width].reshape(token_count, QUERY_HEADS, HEAD_SIZE), cosine_table, sine_table
    ).astype(jnp.bfloat16)
    key_rotated = apply_rotary(
        qkv[:, query_width : query_width + key_width].reshape(
            token_count, KEY_VALUE_HEADS, HEAD_SIZE
        ),
        cosine_table,
        sine_table,
    ).astype(jnp.bfloat16)
    value_rows = (
        qkv[:, query_width + key_width :]
        .astype(jnp.bfloat16)
        .reshape(token_count, KEY_VALUE_HEADS, HEAD_SIZE)
    )
    attn_mix, log_total = attention(query_rotated, key_rotated, value_rows, visible)
    resid_mid = resid_in + matrix_product(attn_mix, out_weight)
    normed_two, inv_rms_two = rms_scale(resid_mid, gain_two)

    normed_pair = group_tokens(normed_two)
    gate_pre = matrix_product(normed_pair, w_gate)
    up_pre = matrix_product(normed_pair, w_up)
    sigma = jax.nn.sigmoid(gate_pre)
    hidden = (gate_pre * sigma * up_pre).astype(jnp.bfloat16)
    grad_down = left_t_product(d_out_pair, hidden).astype(jnp.bfloat16)
    d_hidden = right_t_product(d_out_pair, w_down)
    d_gate = (d_hidden * up_pre * sigma * (1.0 + gate_pre * (1.0 - sigma))).astype(jnp.bfloat16)
    d_up = (d_hidden * gate_pre * sigma).astype(jnp.bfloat16)
    d_normed_part = right_t_product(d_gate, w_gate) + right_t_product(d_up, w_up)
    d_normed_two = group_scatter_sum(d_normed_part, token_count)
    grad_gate = left_t_product(normed_pair, d_gate).astype(jnp.bfloat16)
    grad_up = left_t_product(normed_pair, d_up).astype(jnp.bfloat16)
    down_part = matrix_product(hidden, w_down)
    layer_out = (resid_mid + group_scatter_sum(down_part, token_count)).astype(jnp.bfloat16)

    d_resid_part, grad_gain_two = rms_back(d_normed_two, resid_mid, inv_rms_two, gain_two)
    d_resid_mid = d_out + d_resid_part
    d_mid_b = d_resid_mid.astype(jnp.bfloat16)
    grad_output = left_t_product(attn_mix, d_mid_b)
    d_mix = right_t_product(d_mid_b, out_weight).astype(jnp.bfloat16)
    d_query, d_key, d_value = attention_back(
        query_rotated, key_rotated, value_rows, attn_mix, d_mix, log_total, visible
    )
    d_qkv = jnp.concatenate(
        [
            rotary_backward(d_query, cosine_table, sine_table)
            .reshape(token_count, query_width)
            .astype(jnp.bfloat16),
            rotary_backward(d_key, cosine_table, sine_table)
            .reshape(token_count, key_width)
            .astype(jnp.bfloat16),
            d_value.reshape(token_count, key_width).astype(jnp.bfloat16),
        ],
        axis=1,
    )
    grad_qkv = left_t_product(normed_one, d_qkv)
    d_normed_one = right_t_product(d_qkv, qkv_weight)
    d_resid_first, grad_gain_one = rms_back(d_normed_one, resid_in, inv_rms_one, gain_one)
    tokens_grad = d_resid_mid + d_resid_first

    attn_grads = jnp.concatenate([grad_qkv, grad_output], axis=1).astype(jnp.bfloat16)
    columns = w_gate.shape[1]
    pieces = attn_grads.shape[1] // columns
    owned = [
        attn_grads[:, p * columns : (p + 1) * columns].reshape(group_size, half_width, columns)
        for p in range(pieces)
    ]
    gain_rows = jnp.stack([grad_gain_one, grad_gain_two]).reshape(2, group_size, half_width)
    gain_rows = gain_rows.transpose(1, 0, 2).reshape(group_size, 1, 2 * half_width)
    gain_rows = jnp.pad(
        gain_rows.astype(jnp.bfloat16),
        ((0, 0), (0, 2 * UNIT - 1), (0, columns - 2 * half_width)),
    )
    attn_parts = jnp.concatenate(owned + [gain_rows], axis=1)
    sums = summed_over_replicas(grad_gate, grad_up, grad_down, attn_parts)
    sum_gate, sum_up = sums[:width], sums[width : 2 * width]
    sum_down = sums[2 * width : 3 * width].T
    sum_attn = sums[3 * width : 3 * width + pieces * half_width]
    sum_attn = sum_attn.reshape(pieces, half_width, columns)
    sum_attn = jnp.concatenate([sum_attn[p] for p in range(pieces)], axis=1)
    gain_sums = sums[3 * width + pieces * half_width]

    factor = 1.0 / math.sqrt(
        float(token_count * lax.axis_size("group") * lax.axis_size("replica"))
    )

    def scaled(values):
        return values.astype(jnp.float32) * factor

    gain_sums = scaled(gain_sums)
    sum_attn = scaled(sum_attn)
    return (
        layer_out,
        tokens_grad,
        gain_sums[:half_width],
        sum_attn[:, :query_width],
        sum_attn[:, query_width : query_width + key_width],
        sum_attn[:, query_width + key_width : query_width + 2 * key_width],
        sum_attn[:, query_width + 2 * key_width :],
        gain_sums[half_width : 2 * half_width],
        scaled(sum_gate),
        scaled(sum_up),
        scaled(sum_down),
    )


def solution(mesh):
    in_specs = (
        P(("group", "replica"), None),
        P(("group", "replica"), None),
        P(("group", "replica"), None),
        P("group"),
        P("group", None),
        P("group", None),
        P("group", None),
        P("group", None),
        P("group"),
        P(None, "group"),
        P(None, "group"),
        P("group", None),
    )
    out_specs = (
        P(("group", "replica"), None),
        P(("group", "replica"), None),
        P("group"),
        P("group", None),
        P("group", None),
        P("group", None),
        P("group", None),
        P("group"),
        P(None, "group"),
        P(None, "group"),
        P("group", None),
    )
    return jax.shard_map(local, mesh=mesh, in_specs=in_specs, out_specs=out_specs, check_vma=False)
```

```python
import functools
import math

import jax
import jax.numpy as jnp
from jax import lax
from jax.experimental import pallas as pl
from jax.experimental.pallas import tpu as pltpu
from jax.sharding import PartitionSpec as P

QUERY_HEADS = 15
KEY_VALUE_HEADS = 5
HEAD_SIZE = 64


EPS = 1e-05


def matrix_product(left, right):
    return jnp.dot(left, right, preferred_element_type=jnp.float32)


def left_t_product(left, right):
    return lax.dot_general(
        left, right, (((0,), (0,)), ((), ())), preferred_element_type=jnp.float32
    )


def right_t_product(left, right):
    return lax.dot_general(
        left, right, (((1,), (1,)), ((), ())), preferred_element_type=jnp.float32
    )


def mixed_einsum(form, left, right):
    return jnp.einsum(form, left, right, preferred_element_type=jnp.float32)


def sequence_tables(lengths, token_count):
    ends = jnp.cumsum(lengths)
    starts = ends - lengths
    indices = jnp.arange(token_count, dtype=jnp.int32)
    seq_of = jnp.sum((indices[:, None] >= ends[None, :]).astype(jnp.int32), axis=1)
    onehot = (seq_of[:, None] == jnp.arange(lengths.shape[0], dtype=jnp.int32)[None, :]).astype(
        jnp.int32
    )
    position = indices - jnp.sum(onehot * starts[None, :], axis=1)
    half_dim = HEAD_SIZE // 2
    freqs = 10000.0 ** (-(jnp.arange(half_dim, dtype=jnp.float32) * 2.0 / HEAD_SIZE))
    angles = position.astype(jnp.float32)[:, None] * freqs[None, :]
    visible = (seq_of[:, None] == seq_of[None, :]) & (indices[None, :] <= indices[:, None])
    return (jnp.cos(angles), jnp.sin(angles), visible)


def apply_rotary(values, cosine_table, sine_table):
    half_dim = values.shape[-1] // 2
    first_half = values[..., :half_dim]
    second_half = values[..., half_dim:]
    cos_b = cosine_table[:, None, :]
    sin_b = sine_table[:, None, :]
    return jnp.concatenate(
        [first_half * cos_b - second_half * sin_b, second_half * cos_b + first_half * sin_b],
        axis=-1,
    )


def rotary_backward(values, cosine_table, sine_table):
    half_dim = values.shape[-1] // 2
    first_half = values[..., :half_dim]
    second_half = values[..., half_dim:]
    cos_b = cosine_table[:, None, :]
    sin_b = sine_table[:, None, :]
    return jnp.concatenate(
        [first_half * cos_b + second_half * sin_b, second_half * cos_b - first_half * sin_b],
        axis=-1,
    )


def rms_scale(resid, gain):
    inv_rms = lax.rsqrt(jnp.mean(resid * resid, axis=-1, keepdims=True) + EPS)
    return ((resid * inv_rms * gain.astype(jnp.float32)).astype(jnp.bfloat16), inv_rms)


def rms_back(d_normed, resid, inv_rms, gain):
    scaled = d_normed * gain.astype(jnp.float32)
    d_resid = inv_rms * scaled - resid * inv_rms**3 * jnp.mean(
        scaled * resid, axis=-1, keepdims=True
    )
    d_gain = jnp.sum(d_normed * resid * inv_rms, axis=0)
    return (d_resid, d_gain)


def masked_scores(query_rotated, key_rotated, visible):
    token_count = query_rotated.shape[0]
    query_grouped = query_rotated.reshape(
        token_count, KEY_VALUE_HEADS, QUERY_HEADS // KEY_VALUE_HEADS, HEAD_SIZE
    )
    scores = mixed_einsum("qhgd,khd->hgqk", query_grouped, key_rotated) * (
        1.0 / math.sqrt(HEAD_SIZE)
    )
    return (jnp.where(visible[None, None], scores, -1e30), query_grouped)


def attention(query_rotated, key_rotated, value_row_block, visible):
    token_count = query_rotated.shape[0]
    scores, query_grouped = masked_scores(query_rotated, key_rotated, visible)
    top = jnp.max(scores, axis=-1, keepdims=True)
    expo = jnp.exp(scores - top)
    total = jnp.sum(expo, axis=-1, keepdims=True)
    log_total = top + jnp.log(total)
    probs = (expo / total).astype(jnp.bfloat16)
    mixed = mixed_einsum("hgqk,khd->qhgd", probs, value_row_block)
    return (mixed.reshape(token_count, QUERY_HEADS * HEAD_SIZE).astype(jnp.bfloat16), log_total)


def attention_back(
    query_rotated,
    key_rotated,
    value_row_block,
    attention_mixture,
    mixture_gradient,
    log_total,
    visible,
):
    token_count = query_rotated.shape[0]
    scores, query_grouped = masked_scores(query_rotated, key_rotated, visible)
    weights_f = jnp.exp(scores - log_total)
    probs = weights_f.astype(jnp.bfloat16)
    mixture_gradient_grouped = mixture_gradient.reshape(
        token_count, KEY_VALUE_HEADS, QUERY_HEADS // KEY_VALUE_HEADS, HEAD_SIZE
    )
    mixture_grouped = attention_mixture.reshape(
        token_count, KEY_VALUE_HEADS, QUERY_HEADS // KEY_VALUE_HEADS, HEAD_SIZE
    )
    value_gradient = mixed_einsum("hgqk,qhgd->khd", probs, mixture_gradient_grouped)
    d_probs = mixed_einsum("qhgd,khd->hgqk", mixture_gradient_grouped, value_row_block)
    delta = mixed_einsum("qhgd,qhgd->hgq", mixture_gradient_grouped, mixture_grouped)[..., None]
    d_scores = (weights_f * (d_probs - delta) * (1.0 / math.sqrt(HEAD_SIZE))).astype(jnp.bfloat16)
    d_query = mixed_einsum("hgqk,khd->qhgd", d_scores, key_rotated).reshape(
        token_count, QUERY_HEADS, HEAD_SIZE
    )
    key_gradient = mixed_einsum("hgqk,qhgd->khd", d_scores, query_grouped)
    return (d_query, key_gradient, value_gradient)


def from_member(values, shift):
    size = lax.axis_size("group")
    return lax.ppermute(values, "group", [(j, (j - shift) % size) for j in range(size)])


def to_member(values, shift):
    size = lax.axis_size("group")
    return lax.ppermute(values, "group", [(j, (j + shift) % size) for j in range(size)])


def group_tokens(values):
    others = [from_member(values, k) for k in range(1, lax.axis_size("group"))]
    return jnp.concatenate([values] + others, axis=0)


def group_scatter_sum(parts, token_count):
    total = parts[:token_count]
    for k in range(1, lax.axis_size("group")):
        part = parts[k * token_count : (k + 1) * token_count].astype(jnp.bfloat16)
        total = total + to_member(part, k).astype(jnp.float32)
    return total


def in_group_order(blocks, axis):
    size = len(blocks)
    me = lax.axis_index("group")
    if size == 2:
        first = jnp.where(me == 0, blocks[0], blocks[1])
        second = jnp.where(me == 0, blocks[1], blocks[0])
        return jnp.concatenate([first, second], axis=axis)
    stacked = jnp.roll(jnp.stack(blocks), me, axis=0)
    return jnp.concatenate([stacked[i] for i in range(size)], axis=axis)


def gather_rows(block):
    half = block.shape[0] // 2
    core = lax.rem(lax.axis_index("replica"), 2)
    pairs = [(i, i ^ 1) for i in range(lax.axis_size("replica"))]
    mine = lax.dynamic_slice_in_dim(block, core * half, half, axis=0)
    blocks = [block]
    for k in range(1, lax.axis_size("group")):
        piece = from_member(mine, k)
        pair = lax.ppermute(piece, "replica", pairs)
        first = jnp.where(core == 0, piece, pair)
        second = jnp.where(core == 0, pair, piece)
        blocks.append(jnp.concatenate([first, second], axis=0))
    return in_group_order(blocks, 0)


UNIT = 32
LAG = 6


def replica_layout(replicas):
    chips = replicas // 2
    outer = 4 if chips % 4 == 0 else (2 if chips % 2 == 0 else 1)
    return outer, chips // outer


def sum_kernel(dims, gate_ref, up_ref, down_ref, attn_ref, out_ref, *scratch):
    groups, outer, inner, per_dense, per_attn = dims
    (
        core_in,
        part,
        low_in,
        high_in,
        inner_in,
        group_out,
        group_in,
        core_send,
        core_recv,
        inner_send,
        inner_recv,
        up_send,
        low_recv,
        high_recv,
        fin_low_send,
        fin_high_send,
        fin_inner_send,
        fin_core_send,
        fin_recv,
        fin_core_recv,
        group_send,
        group_recv,
    ) = scratch
    dense = (gate_ref, up_ref, down_ref)
    first_attn = len(dense) * per_dense
    units = first_attn + per_attn
    me = lax.axis_index("replica")
    mine = lax.axis_index("group")
    core = lax.rem(me, 2)
    inner_at = lax.rem(me // 2, inner)
    outer_at = me // (2 * inner)

    def replica_of(o, i, c):
        return {"replica": (o * inner + i) * 2 + c}

    def rows(u):
        return pl.ds(pl.multiple_of(u * UNIT, UNIT), UNIT)

    def pair_rows(u, c):
        return pl.ds(pl.multiple_of((u * 2 + c) * UNIT, UNIT), UNIT)

    def copy(source, target, send, recv, device):
        return pltpu.make_async_remote_copy(
            src_ref=source,
            dst_ref=target,
            send_sem=send,
            recv_sem=recv,
            device_id=device,
            device_id_type=pl.DeviceIdType.MESH,
        )

    other_core = replica_of(outer_at, inner_at, 1 - core)

    def core_copy(source, slot):
        return copy(
            source, core_in.at[rows(slot)], core_send.at[slot], core_recv.at[slot], other_core
        )

    def dense_copy(a, j):
        return core_copy(dense[a].at[pair_rows(j, 1 - core)], a * per_dense + j)

    def attn_slot(owner, j):
        return first_attn + owner * per_attn + j

    def attn_copy(owner, j):
        return core_copy(attn_ref.at[owner, pair_rows(j, 1 - core)], attn_slot(owner, j))

    def group_copy(k, j):
        owner = lax.rem(mine + k, groups)
        return copy(
            group_out.at[k - 1, rows(j)],
            group_in.at[k - 1, rows(j)],
            group_send.at[k - 1, j],
            group_recv.at[k - 1, j],
            {"group": owner},
        )

    def inner_copy(u, owner):
        k = lax.rem(inner_at - owner + inner, inner) - 1
        return copy(
            part.at[rows(u)],
            inner_in.at[k, rows(u)],
            inner_send.at[u],
            inner_recv.at[k, u],
            replica_of(outer_at, owner, core),
        )

    def up_copy(u, step):
        buffer, recv = (low_in, low_recv) if step > 0 else (high_in, high_recv)
        return copy(
            part.at[rows(u)],
            buffer.at[rows(u)],
            up_send.at[u],
            recv.at[u],
            replica_of(outer_at + step, inner_at, core),
        )

    def final_copy(u, send, device):
        place = out_ref.at[pair_rows(u, core)]
        return copy(place, place, send, fin_recv.at[u], device)

    def final_low(u):
        return final_copy(u, fin_low_send.at[u], replica_of(outer_at - 1, inner_at, core))

    def final_high(u):
        return final_copy(u, fin_high_send.at[u], replica_of(outer_at + 1, inner_at, core))

    def final_inner(u, k):
        peer = lax.rem(inner_at + k, inner)
        return final_copy(u, fin_inner_send.at[k - 1, u], replica_of(outer_at, peer, core))

    def final_core(u, c):
        place = out_ref.at[pair_rows(u, c)]
        return copy(place, place, fin_core_send.at[u], fin_core_recv.at[u], other_core)

    def wide(values):
        return values.astype(jnp.float32)

    def add_in(u, arrived):
        part[rows(u)] = (wide(part[rows(u)]) + wide(arrived)).astype(part.dtype)

    def role(u):
        turn, slot = u // 5, lax.rem(u, 5)
        late = slot // 3
        count = turn * 3 + slot
        owner_early = lax.rem(count, inner)
        owner_late = lax.rem(slot + turn, inner)
        root_early = max(outer // 2 - 1, 0) + lax.rem(count // inner, min(outer, 2))
        root_late = lax.rem(turn, outer)
        early = 1 - late
        owner = early * owner_early + late * owner_late
        root = early * root_early + late * root_late
        return early, owner, root

    def facts(u):
        early, owner, root = role(u)
        owns = inner_at == owner
        in_tree = (early == 0) | owns
        at_root = outer_at == root
        tallest = jnp.maximum(root, outer - 1 - root)
        below, above = outer_at < root, outer_at > root
        height = (
            below.astype(jnp.int32) * outer_at
            + above.astype(jnp.int32) * (outer - 1 - outer_at)
            + at_root.astype(jnp.int32) * tallest
        )
        distance = jnp.abs(outer_at - root)
        up_step = early + height
        final_step = 1 + tallest
        down_step = final_step + distance + (1 - owns.astype(jnp.int32))
        return {
            "early": early == 1,
            "owner": owner,
            "owns": owns,
            "in_tree": in_tree,
            "at_root": at_root,
            "below": below,
            "above": above,
            "up_step": up_step,
            "final_step": final_step,
            "down_step": down_step,
            "from_low": (outer_at > 0) & (outer_at <= root),
            "from_high": (outer_at < outer - 1) & (outer_at >= root),
            "sends_inner": (inner_at != owner) & ((early == 1) | at_root),
        }

    barrier = pltpu.get_barrier_semaphore()

    def greet(device):
        pl.semaphore_signal(
            barrier, inc=1, device_id=device, device_id_type=pl.DeviceIdType.MESH
        )

    greet(other_core)
    for k in range(1, inner):
        greet(replica_of(outer_at, lax.rem(inner_at + k, inner), core))
    for k in range(1, groups):
        greet({"group": lax.rem(mine + k, groups)})

    @pl.when(outer_at > 0)
    def _():
        greet(replica_of(outer_at - 1, inner_at, core))

    @pl.when(outer_at < outer - 1)
    def _():
        greet(replica_of(outer_at + 1, inner_at, core))

    ends = (outer_at > 0).astype(jnp.int32) + (outer_at < outer - 1).astype(jnp.int32)
    pl.semaphore_wait(barrier, 1 + (inner - 1) + (groups - 1) + ends)

    @pl.loop(0, per_dense)
    def _(j):
        dense_copy(0, j).start()

    @pl.loop(0, per_attn)
    def _(j):
        for k in range(1, groups):
            attn_copy(lax.rem(mine + k, groups), j).start()

    for a in range(1, len(dense)):

        @pl.loop(0, per_dense)
        def _(j):
            dense_copy(a, j).start()

    @pl.loop(0, per_attn)
    def _(j):
        attn_copy(mine, j).start()

    def first_sum(u):
        for a in range(len(dense)):

            @pl.when((u >= a * per_dense) & (u < (a + 1) * per_dense))
            def _():
                j = u - a * per_dense
                dense_copy(a, j).wait_recv()
                total = wide(dense[a][pair_rows(j, core)]) + wide(core_in[rows(u)])
                part[rows(u)] = total.astype(part.dtype)

        @pl.when(u >= first_attn)
        def _():
            j = u - first_attn
            attn_copy(mine, j).wait_recv()
            total = wide(attn_ref[mine, pair_rows(j, core)]) + wide(
                core_in[rows(attn_slot(mine, j))]
            )
            for k in range(1, groups):
                group_copy(k, j).wait_recv()
                total = total + wide(group_in[k - 1, rows(j)])
            part[rows(u)] = total.astype(part.dtype)

    def to_groups(j):
        for k in range(1, groups):
            owner = lax.rem(mine + k, groups)
            attn_copy(owner, j).wait_recv()
            total = wide(attn_ref[owner, pair_rows(j, core)]) + wide(
                core_in[rows(attn_slot(owner, j))]
            )
            group_out[k - 1, rows(j)] = total.astype(group_out.dtype)
        for k in range(1, groups):
            group_copy(k, j).start()

    def distribute(u, f):
        @pl.when(f["from_low"] & f["in_tree"])
        def _():
            final_low(u).start()

        @pl.when(f["from_high"] & f["in_tree"])
        def _():
            final_high(u).start()

        @pl.when(f["owns"] & (f["early"] | f["at_root"]))
        def _():
            for k in range(1, inner):
                final_inner(u, k).start()

        final_core(u, core).start()

    def gather_inner(u):
        for k in range(1, inner):
            inner_arrival(u, k).wait_recv()
            add_in(u, inner_in[k - 1, rows(u)])

    def inner_arrival(u, k):
        return copy(
            part.at[rows(u)],
            inner_in.at[k - 1, rows(u)],
            inner_send.at[u],
            inner_recv.at[k - 1, u],
            other_core,
        )

    def finish(u, f):
        out_ref[pair_rows(u, core)] = part[rows(u)]
        distribute(u, f)

    def act(u, step):
        f = facts(u)

        @pl.when(step == 0)
        def _():
            first_sum(u)

            @pl.when(f["early"] & (inner_at != f["owner"]))
            def _():
                inner_copy(u, f["owner"]).start()

        @pl.when(f["in_tree"] & (step == f["up_step"]))
        def _():
            @pl.when(f["early"])
            def _():
                gather_inner(u)

            @pl.when(f["from_low"])
            def _():
                up_copy_from(u, 1).wait_recv()
                add_in(u, low_in[rows(u)])

            @pl.when(f["from_high"])
            def _():
                up_copy_from(u, -1).wait_recv()
                add_in(u, high_in[rows(u)])

            @pl.when(f["below"])
            def _():
                up_copy(u, 1).start()

            @pl.when(f["above"])
            def _():
                up_copy(u, -1).start()

            @pl.when(f["at_root"] & jnp.logical_not(f["early"]) & (inner_at != f["owner"]))
            def _():
                inner_copy(u, f["owner"]).start()

        @pl.when(f["at_root"] & f["owns"] & (step == f["final_step"]))
        def _():
            @pl.when(jnp.logical_not(f["early"]))
            def _():
                gather_inner(u)

            finish(u, f)

        @pl.when(jnp.logical_not(f["at_root"] & f["owns"]) & (step == f["down_step"]))
        def _():
            final_core_arrival(u).wait_recv()
            distribute(u, f)

    def up_copy_from(u, step):
        buffer, recv = (low_in, low_recv) if step > 0 else (high_in, high_recv)
        return copy(part.at[rows(u)], buffer.at[rows(u)], up_send.at[u], recv.at[u], other_core)

    def final_core_arrival(u):
        place = out_ref.at[pair_rows(u, core)]
        return copy(place, place, fin_core_send.at[u], fin_recv.at[u], other_core)

    steps = 2 * outer + 2
    first_group_turn = 6

    @pl.loop(0, units + (steps - 1) * LAG)
    def _(t):
        @pl.loop(0, steps)
        def _(step):
            u = t - step * LAG

            @pl.when((u >= 0) & (u < units))
            def _():
                act(u, step)

        @pl.when((t >= first_group_turn) & (t < first_group_turn + per_attn))
        def _():
            to_groups(t - first_group_turn)

    @pl.loop(0, units)
    def _(u):
        f = facts(u)
        final_core(u, 1 - core).wait_recv()
        final_core(u, core).wait_send()

        @pl.when(f["sends_inner"])
        def _():
            inner_copy(u, f["owner"]).wait_send()

        @pl.when(f["in_tree"] & jnp.logical_not(f["at_root"]))
        def _():
            up_copy_from(u, 1).wait_send()

        @pl.when(f["from_low"] & f["in_tree"])
        def _():
            final_low(u).wait_send()

        @pl.when(f["from_high"] & f["in_tree"])
        def _():
            final_high(u).wait_send()

        @pl.when(f["owns"] & (f["early"] | f["at_root"]))
        def _():
            for k in range(1, inner):
                final_inner(u, k).wait_send()

    @pl.loop(0, per_dense)
    def _(j):
        for a in range(len(dense)):
            dense_copy(a, j).wait_send()

    @pl.loop(0, per_attn)
    def _(j):
        for k in range(groups):
            attn_copy(lax.rem(mine + k, groups), j).wait_send()
        for k in range(1, groups):
            group_copy(k, j).wait_send()


def summed_over_replicas(gate, up, down, attn):
    groups = lax.axis_size("group")
    outer, inner = replica_layout(lax.axis_size("replica"))
    columns = gate.shape[1]
    per_dense = gate.shape[0] // (2 * UNIT)
    per_attn = attn.shape[1] // (2 * UNIT)
    units = 3 * per_dense + per_attn
    core_slots = 3 * per_dense + groups * per_attn
    dims = (groups, outer, inner, per_dense, per_attn)

    def held(count, *lead):
        return pltpu.VMEM((*lead, count * UNIT, columns), gate.dtype)

    sems = pltpu.SemaphoreType.DMA
    others = max(inner - 1, 1)
    peers = max(groups - 1, 1)
    vmem = pl.BlockSpec(memory_space=pltpu.VMEM)
    return pl.pallas_call(
        functools.partial(sum_kernel, dims),
        out_shape=jax.ShapeDtypeStruct((units * 2 * UNIT, columns), gate.dtype),
        in_specs=[vmem] * 4,
        out_specs=vmem,
        scratch_shapes=[
            held(core_slots),
            held(units),
            held(units),
            held(units),
            held(units, others),
            held(per_attn, peers),
            held(per_attn, peers),
            sems((core_slots,)),
            sems((core_slots,)),
            sems((units,)),
            sems((others, units)),
            sems((units,)),
            sems((units,)),
            sems((units,)),
            sems((units,)),
            sems((units,)),
            sems((others, units)),
            sems((units,)),
            sems((units,)),
            sems((units,)),
            sems((peers, per_attn)),
            sems((peers, per_attn)),
        ],
        compiler_params=pltpu.CompilerParams(
            collective_id=0, has_side_effects=True, vmem_limit_bytes=67043328
        ),
        name="replica_sum",
    )(gate, up, down, attn)


def local(
    tokens,
    seq_lens,
    cotangent,
    norm1_gain,
    w_query,
    key_weight,
    value_weight,
    w_output,
    norm2_gain,
    w_gate,
    w_up,
    w_down,
):
    token_count, width = tokens.shape
    group = lax.axis_index("group")
    half_width = w_query.shape[0]
    query_width = w_query.shape[1]
    key_width = key_weight.shape[1]
    gains_mine = jnp.stack([norm1_gain, norm2_gain])
    group_size = lax.axis_size("group")
    gains = in_group_order(
        [gains_mine] + [from_member(gains_mine, k) for k in range(1, group_size)], 1
    )
    gain_one, gain_two = gains[0], gains[1]
    qkv_weight = gather_rows(jnp.concatenate([w_query, key_weight, value_weight], axis=1))
    out_weight = gather_rows(w_output)
    d_out = cotangent.astype(jnp.float32)
    d_out_pair = group_tokens(cotangent)

    cosine_table, sine_table, visible = sequence_tables(seq_lens[0], token_count)
    resid_in = tokens.astype(jnp.float32)
    normed_one, inv_rms_one = rms_scale(resid_in, gain_one)
    qkv = matrix_product(normed_one, qkv_weight)
    query_rotated = apply_rotary(
        qkv[:, :query_width].reshape(token_count, QUERY_HEADS, HEAD_SIZE), cosine_table, sine_table
    ).astype(jnp.bfloat16)
    key_rotated = apply_rotary(
        qkv[:, query_width : query_width + key_width].reshape(
            token_count, KEY_VALUE_HEADS, HEAD_SIZE
        ),
        cosine_table,
        sine_table,
    ).astype(jnp.bfloat16)
    value_rows = (
        qkv[:, query_width + key_width :]
        .astype(jnp.bfloat16)
        .reshape(token_count, KEY_VALUE_HEADS, HEAD_SIZE)
    )
    attn_mix, log_total = attention(query_rotated, key_rotated, value_rows, visible)
    resid_mid = resid_in + matrix_product(attn_mix, out_weight)
    normed_two, inv_rms_two = rms_scale(resid_mid, gain_two)

    normed_pair = group_tokens(normed_two)
    gate_pre = matrix_product(normed_pair, w_gate)
    up_pre = matrix_product(normed_pair, w_up)
    sigma = jax.nn.sigmoid(gate_pre)
    hidden = (gate_pre * sigma * up_pre).astype(jnp.bfloat16)
    grad_down = left_t_product(d_out_pair, hidden).astype(jnp.bfloat16)
    d_hidden = right_t_product(d_out_pair, w_down)
    d_gate = (d_hidden * up_pre * sigma * (1.0 + gate_pre * (1.0 - sigma))).astype(jnp.bfloat16)
    d_up = (d_hidden * gate_pre * sigma).astype(jnp.bfloat16)
    d_normed_part = right_t_product(d_gate, w_gate) + right_t_product(d_up, w_up)
    d_normed_two = group_scatter_sum(d_normed_part, token_count)
    grad_gate = left_t_product(normed_pair, d_gate).astype(jnp.bfloat16)
    grad_up = left_t_product(normed_pair, d_up).astype(jnp.bfloat16)
    down_part = matrix_product(hidden, w_down)
    layer_out = (resid_mid + group_scatter_sum(down_part, token_count)).astype(jnp.bfloat16)

    d_resid_part, grad_gain_two = rms_back(d_normed_two, resid_mid, inv_rms_two, gain_two)
    d_resid_mid = d_out + d_resid_part
    d_mid_b = d_resid_mid.astype(jnp.bfloat16)
    grad_output = left_t_product(attn_mix, d_mid_b)
    d_mix = right_t_product(d_mid_b, out_weight).astype(jnp.bfloat16)
    d_query, d_key, d_value = attention_back(
        query_rotated, key_rotated, value_rows, attn_mix, d_mix, log_total, visible
    )
    d_qkv = jnp.concatenate(
        [
            rotary_backward(d_query, cosine_table, sine_table)
            .reshape(token_count, query_width)
            .astype(jnp.bfloat16),
            rotary_backward(d_key, cosine_table, sine_table)
            .reshape(token_count, key_width)
            .astype(jnp.bfloat16),
            d_value.reshape(token_count, key_width).astype(jnp.bfloat16),
        ],
        axis=1,
    )
    grad_qkv = left_t_product(normed_one, d_qkv)
    d_normed_one = right_t_product(d_qkv, qkv_weight)
    d_resid_first, grad_gain_one = rms_back(d_normed_one, resid_in, inv_rms_one, gain_one)
    tokens_grad = d_resid_mid + d_resid_first

    attn_grads = jnp.concatenate([grad_qkv, grad_output], axis=1).astype(jnp.bfloat16)
    columns = w_gate.shape[1]
    pieces = attn_grads.shape[1] // columns
    owned = [
        attn_grads[:, p * columns : (p + 1) * columns].reshape(group_size, half_width, columns)
        for p in range(pieces)
    ]
    gain_rows = jnp.stack([grad_gain_one, grad_gain_two]).reshape(2, group_size, half_width)
    gain_rows = gain_rows.transpose(1, 0, 2).reshape(group_size, 1, 2 * half_width)
    gain_rows = jnp.pad(
        gain_rows.astype(jnp.bfloat16),
        ((0, 0), (0, 2 * UNIT - 1), (0, columns - 2 * half_width)),
    )
    attn_parts = jnp.concatenate(owned + [gain_rows], axis=1)
    sums = summed_over_replicas(grad_gate, grad_up, grad_down, attn_parts)
    sum_gate, sum_up = sums[:width], sums[width : 2 * width]
    sum_down = sums[2 * width : 3 * width].T
    sum_attn = sums[3 * width : 3 * width + pieces * half_width]
    sum_attn = sum_attn.reshape(pieces, half_width, columns)
    sum_attn = jnp.concatenate([sum_attn[p] for p in range(pieces)], axis=1)
    gain_sums = sums[3 * width + pieces * half_width]

    factor = 1.0 / math.sqrt(
        float(token_count * lax.axis_size("group") * lax.axis_size("replica"))
    )

    def scaled(values):
        return values.astype(jnp.float32) * factor

    gain_sums = scaled(gain_sums)
    sum_attn = scaled(sum_attn)
    return (
        layer_out,
        tokens_grad,
        gain_sums[:half_width],
        sum_attn[:, :query_width],
        sum_attn[:, query_width : query_width + key_width],
        sum_attn[:, query_width + key_width : query_width + 2 * key_width],
        sum_attn[:, query_width + 2 * key_width :],
        gain_sums[half_width : 2 * half_width],
        scaled(sum_gate),
        scaled(sum_up),
        scaled(sum_down),
    )


def solution(mesh):
    in_specs = (
        P(("group", "replica"), None),
        P(("group", "replica"), None),
        P(("group", "replica"), None),
        P("group"),
        P("group", None),
        P("group", None),
        P("group", None),
        P("group", None),
        P("group"),
        P(None, "group"),
        P(None, "group"),
        P("group", None),
    )
    out_specs = (
        P(("group", "replica"), None),
        P(("group", "replica"), None),
        P("group"),
        P("group", None),
        P("group", None),
        P("group", None),
        P("group", None),
        P("group"),
        P(None, "group"),
        P(None, "group"),
        P("group", None),
    )
    return jax.shard_map(local, mesh=mesh, in_specs=in_specs, out_specs=out_specs, check_vma=False)
```
